256 devices in a mesh: ctx: 32 (over z, y_lo, core), tp: 8 (over x, y_hi).
Axes of the slice: x: 4, y: 4 (y_hi: 2, y_lo: 2; y = y_hi * 2 + y_lo), z: 8, core: 2. Of those that a mesh axis runs over, the one named last changes fastest.
Arguments:
- queries: bfloat16 [16384, 8192], P('ctx', 'tp'), may hold values from -8 to 8
- stacked_keys: bfloat16 [16384, 1024], P('ctx', 'tp'), may hold values from -8 to 8
- stacked_values: bfloat16 [16384, 1024], P('ctx', 'tp'), may hold values from -6 to 6
- doc_start: int32 [16384], P('ctx'), may hold values from 0 to 16383, as said below
- out_weight: bfloat16 [8192, 4096], P('tp'), may hold values from -0.0625 to 0.0625
Outputs:
- projected: bfloat16 [16384, 4096], P('ctx', 'tp')
The draws below stay inside these ranges and needn't reach their ends.
Inputs may be any that keep to these rules, and one draw needn't show every extreme that they name: doc_start[t] is the position of the first token of the document holding token t; documents are contiguous runs of 1 to 8192 tokens, one document holds exactly 8192 tokens and does not begin at the first of a device's rows, and the last token forms a document of its own.
All inputs are finite; a program needn't handle non-finite values.
Results may differ from the reference program's by a relative error of at most 0.014.
Values may be sent and summed in bfloat16 or wider, within the bound.
A program may use at most 64 MiB of HBM per device.

```python
import math
import jax
import jax.numpy as jnp
from jax import lax

QUERY_HEADS = 64
KEY_VALUE_HEADS = 8
HEAD_WIDTH = 128
DOUT = 4096
CONTEXT_ROWS = 512
PACKED_TOKENS = 16384
SPAN = 16
L_MAX = 8192
N_TP = 8


def draw_queries(key, part):
    complete_shape = (PACKED_TOKENS, QUERY_HEADS * HEAD_WIDTH)
    base = 2.5 * jax.random.normal(jax.random.fold_in(key, 21), complete_shape, jnp.float32)
    return jnp.clip(base, -8.0, 8.0).astype(jnp.bfloat16)


def draw_stacked_keys(key, part):
    complete_shape = (PACKED_TOKENS, KEY_VALUE_HEADS * HEAD_WIDTH)
    base = jax.random.normal(jax.random.fold_in(key, 31), complete_shape, jnp.float32)
    return jnp.clip(base, -8.0, 8.0).astype(jnp.bfloat16)


def draw_doc_start(key, part):
    first_key, second_key, third_key, fourth_key = jax.random.split(key, 4)
    free_blocks = (PACKED_TOKENS - L_MAX) // CONTEXT_ROWS
    lead = jax.random.randint(first_key, (), 0, free_blocks - 1) * CONTEXT_ROWS + jax.random.randint(second_key, (), 1, CONTEXT_ROWS)
    limit = 2 * PACKED_TOKENS + 2 * L_MAX

    def bounded_add(left, right):
        return jnp.minimum(left + right, limit)
    lengths_a = jax.random.randint(third_key, (PACKED_TOKENS,), 1, L_MAX + 1)
    lengths_b = jax.random.randint(fourth_key, (PACKED_TOKENS,), 1, L_MAX + 1)
    ends_a = lax.associative_scan(bounded_add, lengths_a)
    ends_b = lax.associative_scan(bounded_add, lengths_b)
    starts_a = jnp.concatenate([jnp.zeros((1,), jnp.int32), ends_a[:-1].astype(jnp.int32)])
    starts_b = lead + L_MAX + jnp.concatenate([jnp.zeros((1,), jnp.int32), ends_b[:-1].astype(jnp.int32)])
    places = jnp.arange(PACKED_TOKENS, dtype=jnp.int32)
    index_a = jnp.searchsorted(starts_a, places, side='right') - 1
    index_b = jnp.maximum(jnp.searchsorted(starts_b, places, side='right') - 1, 0)
    first_a = starts_a[index_a]
    first_b = starts_b[index_b]
    result = jnp.where(places < lead, first_a, jnp.where(places < lead + L_MAX, lead, first_b))
    result = jnp.where(places == PACKED_TOKENS - 1, PACKED_TOKENS - 1, result)
    return result.astype(jnp.int32)


def shard_levels(own_key, shape, cuts, least, largest):
    level, own = 1.0, jax.random.fold_in(own_key, 6)
    for position, blocks in cuts:
        steps = jnp.exp(jax.random.uniform(jax.random.fold_in(own, position), (blocks,), jnp.float32, least / len(cuts), largest / len(cuts)))
        level = level * jnp.repeat(steps, shape[position] // blocks).reshape([-1 if axis == position else 1 for axis in range(len(shape))])
    return level


def centred(stream_key, extent, deviation, most, cuts=(), kind=jnp.bfloat16):
    array = deviation * jax.random.normal(stream_key, extent, jnp.float32)
    if cuts:
        array = array * shard_levels(stream_key, extent, cuts, -0.22, 0.18)
    return jnp.clip(array, -most, most).astype(kind)


def setup_inputs(seed: int = 0) -> dict:
    keys = jax.random.split(jax.random.key(seed), 6)
    queries = draw_queries(jax.random.fold_in(keys[5], 71), 0)
    stacked_keys = draw_stacked_keys(jax.random.fold_in(keys[5], 71), 0)
    stacked_values = centred(keys[2], (PACKED_TOKENS, KEY_VALUE_HEADS * HEAD_WIDTH), 1.0, 6.0, ((0, 32), (1, 8)))
    doc_start = draw_doc_start(jax.random.fold_in(keys[5], 71), 0)
    out_weight = centred(keys[4], (QUERY_HEADS * HEAD_WIDTH, DOUT), (QUERY_HEADS * HEAD_WIDTH) ** -0.5, 0.0625, ((0, 8),))
    return dict(queries=queries, stacked_keys=stacked_keys, stacked_values=stacked_values, doc_start=doc_start, out_weight=out_weight)


def reference(queries, stacked_keys, stacked_values, doc_start, out_weight):
    queries_per_group = QUERY_HEADS // KEY_VALUE_HEADS
    padding_rows = SPAN * CONTEXT_ROWS
    window_span = padding_rows + CONTEXT_ROWS
    score_scale = 1.0 / math.sqrt(HEAD_WIDTH)
    keys_with_padding = jnp.concatenate([jnp.zeros((padding_rows, KEY_VALUE_HEADS * HEAD_WIDTH), stacked_keys.dtype), stacked_keys], 0)
    values_with_padding = jnp.concatenate([jnp.zeros((padding_rows, KEY_VALUE_HEADS * HEAD_WIDTH), stacked_values.dtype), stacked_values], 0)

    def one_block(block_index):
        first_row = (block_index * CONTEXT_ROWS).astype(jnp.int32)
        query_tile = lax.dynamic_slice_in_dim(queries, first_row, CONTEXT_ROWS, 0).astype(jnp.float32)
        query_tile = query_tile.reshape(CONTEXT_ROWS, KEY_VALUE_HEADS, queries_per_group, HEAD_WIDTH)
        key_tile = lax.dynamic_slice_in_dim(keys_with_padding, first_row, window_span, 0).astype(jnp.float32)
        key_tile = key_tile.reshape(window_span, KEY_VALUE_HEADS, HEAD_WIDTH)
        value_tile = lax.dynamic_slice_in_dim(values_with_padding, first_row, window_span, 0).astype(jnp.float32)
        value_tile = value_tile.reshape(window_span, KEY_VALUE_HEADS, HEAD_WIDTH)
        starts = lax.dynamic_slice_in_dim(doc_start, first_row, CONTEXT_ROWS, 0)
        query_pos = first_row + jnp.arange(CONTEXT_ROWS, dtype=jnp.int32)
        key_pos = first_row - padding_rows + jnp.arange(window_span, dtype=jnp.int32)
        visible = (key_pos[None, :] >= starts[:, None]) & (key_pos[None, :] <= query_pos[:, None])

        def single_head(kv_head):
            query_head = lax.dynamic_index_in_dim(query_tile, kv_head, 1, keepdims=False)
            key_head = lax.dynamic_index_in_dim(key_tile, kv_head, 1, keepdims=False)
            value_head = lax.dynamic_index_in_dim(value_tile, kv_head, 1, keepdims=False)
            scores = jnp.einsum('qgd,kd->gqk', query_head, key_head) * score_scale
            scores = jnp.where(visible[None], scores, -jnp.inf)
            row_max = lax.optimization_barrier(jnp.max(scores, axis=-1, keepdims=True))
            weights = jnp.where(visible[None], jnp.exp(scores - row_max), 0.0)
            rounded = lax.optimization_barrier(weights.astype(jnp.bfloat16)).astype(jnp.float32)
            weighted_sum = jnp.einsum('gqk,kd->gqd', rounded, value_head)
            return (weighted_sum / lax.optimization_barrier(jnp.sum(weights, axis=-1, keepdims=True))).astype(jnp.bfloat16)
        head_outputs = lax.map(single_head, jnp.arange(KEY_VALUE_HEADS, dtype=jnp.int32))
        return head_outputs.transpose(2, 0, 1, 3).reshape(CONTEXT_ROWS, QUERY_HEADS * HEAD_WIDTH)
    attended = lax.map(one_block, jnp.arange(PACKED_TOKENS // CONTEXT_ROWS, dtype=jnp.int32)).reshape(PACKED_TOKENS, QUERY_HEADS * HEAD_WIDTH)
    head_cols = QUERY_HEADS * HEAD_WIDTH // N_TP

    def add_group(index, summed):
        first_col = (index * head_cols).astype(jnp.int32)
        columns = lax.dynamic_slice_in_dim(attended, first_col, head_cols, 1)
        weight_rows = lax.dynamic_slice_in_dim(out_weight, first_col, head_cols, 0)
        partial_value = jnp.dot(columns, weight_rows, preferred_element_type=jnp.float32)
        return summed + lax.optimization_barrier(partial_value.astype(jnp.bfloat16)).astype(jnp.float32)
    summed = lax.fori_loop(0, N_TP, add_group, jnp.zeros((PACKED_TOKENS, DOUT), jnp.float32))
    return summed.astype(jnp.bfloat16)
```

```python
import functools
import math

import jax
import jax.numpy as jnp
from jax import lax
from jax.experimental import pallas as pl
from jax.experimental.pallas import tpu as pltpu

HEAD = 128
HEADS = 8
ROWS = 512
CHUNK = 128
CHUNKS = ROWS // CHUNK
WIDE = CHUNK * HEADS
PAIR = 2 * ROWS
VROWS = 144
ACC = 136
COLS = 512
TAIL = 4
SCALE = math.log2(math.e) / math.sqrt(HEAD)
BIG = 1e30
BF16 = jnp.bfloat16
F32 = jnp.float32
MESH = pl.DeviceIdType.MESH


def kernel(q_hbm, k_ref, v_ref, ds_ref, w_hbm, out_ref, q_buf, w_buf, qs, k_own, v_own, v_raw, kb, vb,
           s_buf, m_ref, acc, att, part, ra, rb, cb, rc, fb, local_sem, kv_send, kv_recv, rs_send, rs_recv):
    i = lax.axis_index("ctx")
    t = lax.axis_index("tp")
    z = i // 4
    yl = (i // 2) % 2
    c = i % 2
    x = t // 2
    yh = t % 2
    z_next = {"ctx": (i + 4) % 32}
    z_prev = {"ctx": (i + 28) % 32}
    core = {"ctx": i + 1 - 2 * c}
    y_mate = {"ctx": i + 2 - 4 * yl}
    x_next = {"tp": (t + 2) % 8}
    x_prev = {"tp": (t + 6) % 8}
    yh_mate = {"tp": t + 1 - 2 * yh}

    load_q = pltpu.make_async_copy(q_hbm, q_buf, local_sem.at[0])
    load_w = pltpu.make_async_copy(w_hbm, w_buf, local_sem.at[1])
    load_q.start()
    load_w.start()

    barrier = pltpu.get_barrier_semaphore()
    for mate in (z_next, z_prev, core, y_mate, x_next, x_prev, yh_mate):
        pl.semaphore_signal(barrier, inc=1, device_id=mate, device_id_type=MESH)

    last = ds_ref[CHUNKS - 1:CHUNKS, CHUNK - 1:CHUNK] - i * ROWS
    kf = k_ref[...].astype(F32)
    keep_rows = lax.broadcasted_iota(jnp.int32, (ROWS, HEAD), 0) >= last
    k_own[...] = jnp.where(keep_rows, kf, kf[ROWS - 1:ROWS, :]).astype(BF16)
    vt = v_ref[...].T
    keep_cols = lax.broadcasted_iota(jnp.int32, (HEAD, ROWS), 1) >= last
    v_own[0:HEAD, :] = jnp.where(keep_cols, vt.astype(F32), 0.0).astype(BF16)
    v_own[HEAD:VROWS, :] = jnp.where(keep_cols[0:VROWS - HEAD, :], 1.0, 0.0).astype(BF16)
    v_raw[0:HEAD, :] = vt
    v_raw[HEAD:VROWS, :] = jnp.ones((VROWS - HEAD, ROWS), BF16)

    pl.semaphore_wait(barrier, 7)

    def half(slot, h):
        off = pl.multiple_of(h * ROWS, ROWS)
        return kb.at[slot, pl.ds(off, ROWS), :], vb.at[slot, :, pl.ds(off, ROWS)]

    def message(src, slot, h, number, mate):
        dst = half(slot, h)
        return [
            pltpu.make_async_remote_copy(
                src_ref=src[n], dst_ref=dst[n], send_sem=kv_send.at[2 * number + n],
                recv_sem=kv_recv.at[2 * number + n], device_id=mate, device_id_type=MESH)
            for n in range(2)
        ]

    def send(src, slot, h, number, mate):
        for copy in message(src, slot, h, number, mate):
            copy.start()

    def arrived(slot, h, number):
        for copy in message(half(slot, h), slot, h, number, core):
            copy.wait_recv()

    own = (k_own, v_own)
    send(own, yl, c, 0, z_next)

    @pl.when(yl == 0)
    def _():
        send(own, 7, c, 11, y_mate)

    @pl.when(c == 0)
    def _():
        send(own, 6, 0, 7, core)

    def relay(dz):
        if dz == 4:
            arrived(6, c, 3)

            @pl.when(c == 1)
            def _():
                send(half(6, 1), 6, 1, 7, core)

            @pl.when(yl == 1)
            def _():
                send(half(6, c), 7, c, 11, y_mate)
            return
        slot = 2 * (dz - 1) + yl
        arrived(slot, c, dz - 1)
        src = half(slot, c)
        send(src, 6 if dz == 3 else slot + 2, c, dz, z_next)
        send(src, slot, c, 3 + dz, core)
        send(src, slot, c, 7 + dz, y_mate)

    def relay_y(dz):
        slot = 7 if dz == 4 else 2 * (dz - 1) + 1 - yl
        arrived(slot, c, 7 + dz)
        send(half(slot, c), slot, c, 11 + dz, core)

    def ready(step):
        if step == 6:
            arrived(6, 1 - c, 7)
        elif step == 7:
            arrived(7, 1 - c, 15)
        elif step % 2 == 0:
            arrived(step + yl, 1 - c, 4 + step // 2)
        else:
            arrived(step - yl, 1 - c, 12 + step // 2)

    def slot_of(step):
        b = step % 2
        return (step // 2) * 2 + yl + b - 2 * yl * b

    def ends_of(step):
        b = step % 2
        block = (z - 1 - step // 2) * 4 + 2 * (yl + b - 2 * yl * b)
        return block * ROWS + ROWS - 1, block * ROWS + 2 * ROWS - 1

    ends_6 = ((i - c) * ROWS - 16 * ROWS * (1 - c) + ROWS - 1, (i - c + 1 - 16) * ROWS + ROWS - 1)
    block_7 = z * 4 * yl + (z * 4 - 14) * (1 - yl)
    ends_7 = (block_7 * ROWS + ROWS - 1, block_7 * ROWS + 2 * ROWS - 1)

    def wide(row):
        return jnp.concatenate([row] * HEADS, axis=1)

    load_q.wait()
    for r in range(CHUNKS):
        for h in range(HEADS):
            scaled = q_buf[r * CHUNK:(r + 1) * CHUNK, h * HEAD:(h + 1) * HEAD].astype(F32) * SCALE
            high = scaled.astype(BF16)
            low = (scaled - high.astype(F32)).astype(BF16)
            rows = slice(r * WIDE + h * HEAD, r * WIDE + (h + 1) * HEAD)
            qs[rows, 0:HEAD] = high
            qs[rows, HEAD:2 * HEAD] = low

    def products(keys, r):
        rows = pl.ds(pl.multiple_of(r * WIDE, WIDE), WIDE)
        return lax.dot_general(jnp.concatenate([keys, keys], axis=1), qs[rows, :],
                               (((1,), (1,)), ((), ())), preferred_element_type=F32)

    for r in range(CHUNKS):
        count = (r + 1) * CHUNK
        cols = slice(r * WIDE, (r + 1) * WIDE)
        s = products(k_ref[0:count, :], r)
        key_at = lax.broadcasted_iota(jnp.int32, (count, CHUNK), 0)
        query_at = lax.broadcasted_iota(jnp.int32, (count, CHUNK), 1) + r * CHUNK
        visible = (key_at >= ds_ref[r:r + 1, :] - i * ROWS) & (key_at <= query_at)
        s = jnp.where(jnp.concatenate([visible] * HEADS, axis=1), s, -BIG)
        m = jnp.max(s, axis=0, keepdims=True)
        p = jnp.exp2(s - m).astype(BF16)
        m_ref[:, cols] = m
        acc[:, cols] = jnp.dot(v_raw[0:ACC, 0:count], p, preferred_element_type=F32)

    def scores(slot, r, b):
        s_buf[b] = products(kb[slot], r)

    def update(slot, r, b, ends):
        cols = pl.ds(pl.multiple_of(r * WIDE, WIDE), WIDE)
        starts = ds_ref[pl.ds(r, 1), :]
        off0 = wide(jnp.where(starts <= ends[0], 0.0, BIG))
        off1 = wide(jnp.where(starts <= ends[1], 0.0, BIG))
        s0 = s_buf[b, 0:ROWS, :]
        s1 = s_buf[b, ROWS:PAIR, :]
        m_old = m_ref[:, cols]
        top = jnp.maximum(jnp.max(s0, axis=0, keepdims=True) - off0, jnp.max(s1, axis=0, keepdims=True) - off1)
        m = jnp.maximum(m_old, top)
        m_ref[:, cols] = m
        p0 = jnp.exp2(s0 - (m + off0)).astype(BF16)
        p1 = jnp.exp2(s1 - (m + off1)).astype(BF16)
        p = jnp.concatenate([p0, p1], axis=0)
        new = jnp.dot(vb[slot, 0:ACC, :], p, preferred_element_type=F32)
        acc[:, cols] = acc[:, cols] * jnp.exp2(m_old - m) + new

    relay(1)
    ready(0)
    scores(slot_of(0), 0, 0)

    steps = 8 - TAIL

    @pl.loop(0, 2 * steps)
    def _(hs):
        step = hs // 2
        odd = hs % 2

        for n in range(steps):
            @pl.when(hs == 2 * n + 1)
            def _(n=n):
                if n <= 3:
                    relay_y(n + 1)
                if n <= 2:
                    relay(n + 2)
                ready(n + 1)

        slot = slot_of(step)
        ends = ends_of(step)
        scores(slot, 2 * odd + 1, 1)
        update(slot, 2 * odd, 0, ends)
        scores(slot_of(step + odd), 2 - 2 * odd, 0)
        update(slot, 2 * odd + 1, 1, ends)

    def tail_step(step):
        if step == 6:
            return 6, ends_6
        if step == 7:
            return 7, ends_7
        return slot_of(step), ends_of(step)

    def rs_copy(src, dst, number, mate):
        return pltpu.make_async_remote_copy(
            src_ref=src, dst_ref=dst, send_sem=rs_send.at[number], recv_sem=rs_recv.at[number],
            device_id=mate, device_id_type=MESH)

    far = (x + 2) % 4
    after = (x + 1) % 4
    before = (x + 3) % 4

    def first(r):
        return (rs_copy(part.at[r, 2 * far + 1], ra.at[r, 0], 5 * r, x_next),
                rs_copy(part.at[r, 2 * far], ra.at[r, 1], 5 * r + 1, x_prev))

    def second(r):
        return (rs_copy(part.at[r, pl.ds(2 * after, 2)], rb.at[r, 0], 5 * r + 2, x_next),
                rs_copy(part.at[r, pl.ds(2 * before, 2)], rb.at[r, 1], 5 * r + 3, x_prev))

    def third(r):
        return rs_copy(cb.at[r], rc.at[r], 5 * r + 4, yh_mate)

    def pass_first(r):
        got = first(r)
        onward = second(r)
        for n, block in ((0, 2 * after + 1), (1, 2 * before)):
            got[n].wait_recv()
            part[r, block] = (part[r, block].astype(F32) + ra[r, n].astype(F32)).astype(BF16)
            onward[n].start()

    def pass_second(r):
        for copy in second(r):
            copy.wait_recv()
        for keep in range(2):
            block = yh if keep else 1 - yh
            total = (part[r, 2 * x + block].astype(F32) + rb[r, 0, block].astype(F32)
                     + rb[r, 1, block].astype(F32))
            if keep:
                fb[r] = total
            else:
                cb[r] = total.astype(BF16)
                third(r).start()

    def pass_third(r):
        third(r).wait_recv()
        rows = pl.ds(pl.multiple_of(r * CHUNK, CHUNK), CHUNK)
        out_ref[rows, :] = (fb[r] + rc[r].astype(F32)).astype(BF16)

    load_w.wait()

    @pl.loop(0, CHUNKS)
    def _(r):
        for n in range(TAIL):
            step = 8 - TAIL + n
            if n < TAIL - 1:
                @pl.when(r == 0)
                def _():
                    ready(step + 1)
                scores(tail_step(step + 1)[0], r, (n + 1) % 2)
            else:
                scores(tail_step(8 - TAIL)[0], (r + 1) % CHUNKS, 0)
            slot, ends = tail_step(step)
            update(slot, r, n % 2, ends)

        @pl.when(r >= 1)
        def _():
            pass_first(r - 1)

        cols = pl.ds(pl.multiple_of(r * WIDE, WIDE), WIDE)
        done = (acc[0:HEAD, cols] / acc[HEAD:HEAD + 1, cols]).astype(BF16)
        for h in range(HEADS):
            att[:, h * HEAD:(h + 1) * HEAD] = done[:, h * CHUNK:(h + 1) * CHUNK].T
        for block in range(8):
            part[r, block] = jnp.dot(att[...], w_buf[:, block * COLS:(block + 1) * COLS],
                                     preferred_element_type=F32).astype(BF16)
        for copy in first(r):
            copy.start()

        @pl.when(r >= 2)
        def _():
            pass_second(r - 2)

    pass_first(CHUNKS - 1)
    pass_second(CHUNKS - 2)
    pass_third(0)
    pass_third(1)
    pass_second(CHUNKS - 1)
    pass_third(2)
    pass_third(3)

    for number in range(16):
        for copy in message(own, 0, 0, number, core):
            copy.wait_send()
    for r in range(CHUNKS):
        for copy in (*first(r), *second(r), third(r)):
            copy.wait_send()


def local(queries, stacked_keys, stacked_values, doc_start, out_weight):
    vmem = pl.BlockSpec(memory_space=pltpu.VMEM)
    anywhere = pl.BlockSpec(memory_space=pl.ANY)
    return pl.pallas_call(
        kernel,
        out_shape=jax.ShapeDtypeStruct((ROWS, COLS), BF16),
        in_specs=[anywhere, vmem, vmem, vmem, anywhere],
        out_specs=vmem,
        scratch_shapes=[
            pltpu.VMEM((ROWS, HEADS * HEAD), BF16),
            pltpu.VMEM((HEADS * HEAD, 8 * COLS), BF16),
            pltpu.VMEM((CHUNKS * WIDE, 2 * HEAD), BF16),
            pltpu.VMEM((ROWS, HEAD), BF16),
            pltpu.VMEM((VROWS, ROWS), BF16),
            pltpu.VMEM((VROWS, ROWS), BF16),
            pltpu.VMEM((8, PAIR, HEAD), BF16),
            pltpu.VMEM((8, VROWS, PAIR), BF16),
            pltpu.VMEM((2, PAIR, WIDE), F32),
            pltpu.VMEM((1, CHUNKS * WIDE), F32),
            pltpu.VMEM((ACC, CHUNKS * WIDE), F32),
            pltpu.VMEM((CHUNK, HEADS * HEAD), BF16),
            pltpu.VMEM((CHUNKS, 8, CHUNK, COLS), BF16),
            pltpu.VMEM((CHUNKS, 2, CHUNK, COLS), BF16),
            pltpu.VMEM((CHUNKS, 2, 2, CHUNK, COLS), BF16),
            pltpu.VMEM((CHUNKS, CHUNK, COLS), BF16),
            pltpu.VMEM((CHUNKS, CHUNK, COLS), BF16),
            pltpu.VMEM((CHUNKS, CHUNK, COLS), F32),
            pltpu.SemaphoreType.DMA((2,)),
            pltpu.SemaphoreType.DMA((32,)),
            pltpu.SemaphoreType.DMA((32,)),
            pltpu.SemaphoreType.DMA((5 * CHUNKS,)),
            pltpu.SemaphoreType.DMA((5 * CHUNKS,)),
        ],
        compiler_params=pltpu.CompilerParams(
            collective_id=0, has_side_effects=True, vmem_limit_bytes=60 << 20),
        name="attend_and_project",
    )(queries, stacked_keys, stacked_values, doc_start.reshape(CHUNKS, CHUNK), out_weight)


def solution(mesh):
    from jax.sharding import PartitionSpec as P

    return jax.shard_map(
        local,
        mesh=mesh,
        in_specs=(P("ctx", "tp"), P("ctx", "tp"), P("ctx", "tp"), P("ctx"), P("tp", None)),
        out_specs=P("ctx", "tp"),
        check_vma=False,
    )
```

```python
import functools
import math

import jax
import jax.numpy as jnp
from jax import lax
from jax.experimental import pallas as pl
from jax.experimental.pallas import tpu as pltpu

HEAD = 128
HEADS = 8
ROWS = 512
CHUNK = 128
CHUNKS = ROWS // CHUNK
WIDE = CHUNK * HEADS
PAIR = 2 * ROWS
VROWS = 144
ACC = 136
COLS = 512
TAIL = 4
SCALE = math.log2(math.e) / math.sqrt(HEAD)
BIG = 1e30
BF16 = jnp.bfloat16
F32 = jnp.float32
MESH = pl.DeviceIdType.MESH


def kernel(q_hbm, k_ref, v_ref, ds_ref, w_hbm, out_ref, q_buf, w_buf, qs, k_own, v_own, v_raw, kb, vb,
           s_buf, m_ref, acc, att, part, ra, rb, cb, rc, fb, local_sem, kv_send, kv_recv, rs_send, rs_recv):
    i = lax.axis_index("ctx")
    t = lax.axis_index("tp")
    z = i // 4
    yl = (i // 2) % 2
    c = i % 2
    x = t // 2
    yh = t % 2
    z_next = {"ctx": (i + 4) % 32}
    z_prev = {"ctx": (i + 28) % 32}
    core = {"ctx": i + 1 - 2 * c}
    y_mate = {"ctx": i + 2 - 4 * yl}
    x_next = {"tp": (t + 2) % 8}
    x_prev = {"tp": (t + 6) % 8}
    yh_mate = {"tp": t + 1 - 2 * yh}

    load_q = pltpu.make_async_copy(q_hbm, q_buf, local_sem.at[0])
    load_w = pltpu.make_async_copy(w_hbm, w_buf, local_sem.at[1])
    load_q.start()
    load_w.start()

    barrier = pltpu.get_barrier_semaphore()
    for mate in (z_next, z_prev, core, y_mate, x_next, x_prev, yh_mate):
        pl.semaphore_signal(barrier, inc=1, device_id=mate, device_id_type=MESH)

    last = ds_ref[CHUNKS - 1:CHUNKS, CHUNK - 1:CHUNK] - i * ROWS
    kf = k_ref[...].astype(F32)
    keep_rows = lax.broadcasted_iota(jnp.int32, (ROWS, HEAD), 0) >= last
    k_own[...] = jnp.where(keep_rows, kf, kf[ROWS - 1:ROWS, :]).astype(BF16)
    vt = v_ref[...].T
    keep_cols = lax.broadcasted_iota(jnp.int32, (HEAD, ROWS), 1) >= last
    v_own[0:HEAD, :] = jnp.where(keep_cols, vt.astype(F32), 0.0).astype(BF16)
    v_own[HEAD:VROWS, :] = jnp.where(keep_cols[0:VROWS - HEAD, :], 1.0, 0.0).astype(BF16)
    v_raw[0:HEAD, :] = vt
    v_raw[HEAD:VROWS, :] = jnp.ones((VROWS - HEAD, ROWS), BF16)

    pl.semaphore_wait(barrier, 7)

    def half(slot, h):
        off = pl.multiple_of(h * ROWS, ROWS)
        return kb.at[slot, pl.ds(off, ROWS), :], vb.at[slot, :, pl.ds(off, ROWS)]

    def part_copy(src, slot, h, number, mate, n):
        return pltpu.make_async_remote_copy(
            src_ref=src[n], dst_ref=half(slot, h)[n], send_sem=kv_send.at[2 * number + n],
            recv_sem=kv_recv.at[2 * number + n], device_id=mate, device_id_type=MESH)

    def send_part(src, slot, h, number, mate, n):
        part_copy(src, slot, h, number, mate, n).start()

    def send(src, slot, h, number, mate):
        for n in range(2):
            send_part(src, slot, h, number, mate, n)

    def arrived(slot, h, number, n):
        part_copy(half(slot, h), slot, h, number, core, n).wait_recv()

    own = (k_own, v_own)
    send(own, yl, c, 0, z_next)

    @pl.when(yl == 0)
    def _():
        send(own, 7, c, 11, y_mate)

    @pl.when(c == 0)
    def _():
        send(own, 6, 0, 7, core)

    def relay(dz):
        for n in range(2):
            if dz == 4:
                arrived(6, c, 3, n)

                @pl.when(c == 1)
                def _(n=n):
                    send_part(half(6, 1), 6, 1, 7, core, n)

                @pl.when(yl == 1)
                def _(n=n):
                    send_part(half(6, c), 7, c, 11, y_mate, n)
                continue
            slot = 2 * (dz - 1) + yl
            arrived(slot, c, dz - 1, n)
            src = half(slot, c)
            send_part(src, 6 if dz == 3 else slot + 2, c, dz, z_next, n)
            send_part(src, slot, c, 3 + dz, core, n)
            send_part(src, slot, c, 7 + dz, y_mate, n)

    def relay_y(dz):
        slot = 7 if dz == 4 else 2 * (dz - 1) + 1 - yl
        for n in range(2):
            arrived(slot, c, 7 + dz, n)
            send_part(half(slot, c), slot, c, 11 + dz, core, n)

    def ready(step, n):
        if step == 6:
            arrived(6, 1 - c, 7, n)
        elif step == 7:
            arrived(7, 1 - c, 15, n)
        elif step % 2 == 0:
            arrived(step + yl, 1 - c, 4 + step // 2, n)
        else:
            arrived(step - yl, 1 - c, 12 + step // 2, n)

    def slot_of(step):
        b = step % 2
        return (step // 2) * 2 + yl + b - 2 * yl * b

    def ends_of(step):
        b = step % 2
        block = (z - 1 - step // 2) * 4 + 2 * (yl + b - 2 * yl * b)
        return block * ROWS + ROWS - 1, block * ROWS + 2 * ROWS - 1

    ends_6 = ((i - c) * ROWS - 16 * ROWS * (1 - c) + ROWS - 1, (i - c + 1 - 16) * ROWS + ROWS - 1)
    block_7 = z * 4 * yl + (z * 4 - 14) * (1 - yl)
    ends_7 = (block_7 * ROWS + ROWS - 1, block_7 * ROWS + 2 * ROWS - 1)

    def wide(row):
        return jnp.concatenate([row] * HEADS, axis=1)

    load_q.wait()
    for r in range(CHUNKS):
        for h in range(HEADS):
            scaled = q_buf[r * CHUNK:(r + 1) * CHUNK, h * HEAD:(h + 1) * HEAD].astype(F32) * SCALE
            high = scaled.astype(BF16)
            low = (scaled - high.astype(F32)).astype(BF16)
            rows = slice(r * WIDE + h * HEAD, r * WIDE + (h + 1) * HEAD)
            qs[rows, 0:HEAD] = high
            qs[rows, HEAD:2 * HEAD] = low

    def products(keys, r):
        rows = pl.ds(pl.multiple_of(r * WIDE, WIDE), WIDE)
        return lax.dot_general(jnp.concatenate([keys, keys], axis=1), qs[rows, :],
                               (((1,), (1,)), ((), ())), preferred_element_type=F32)

    for r in range(CHUNKS):
        count = (r + 1) * CHUNK
        cols = slice(r * WIDE, (r + 1) * WIDE)
        s = products(k_ref[0:count, :], r)
        key_at = lax.broadcasted_iota(jnp.int32, (count, CHUNK), 0)
        query_at = lax.broadcasted_iota(jnp.int32, (count, CHUNK), 1) + r * CHUNK
        visible = (key_at >= ds_ref[r:r + 1, :] - i * ROWS) & (key_at <= query_at)
        s = jnp.where(jnp.concatenate([visible] * HEADS, axis=1), s, -BIG)
        m = jnp.max(s, axis=0, keepdims=True)
        p = jnp.exp2(s - m).astype(BF16)
        m_ref[:, cols] = m
        acc[:, cols] = jnp.dot(v_raw[0:ACC, 0:count], p, preferred_element_type=F32)

    def scores(slot, r, b):
        s_buf[b] = products(kb[slot], r)

    def update(slot, r, b, ends):
        cols = pl.ds(pl.multiple_of(r * WIDE, WIDE), WIDE)
        starts = ds_ref[pl.ds(r, 1), :]
        off0 = wide(jnp.where(starts <= ends[0], 0.0, BIG))
        off1 = wide(jnp.where(starts <= ends[1], 0.0, BIG))
        s0 = s_buf[b, 0:ROWS, :]
        s1 = s_buf[b, ROWS:PAIR, :]
        m_old = m_ref[:, cols]
        top = jnp.maximum(jnp.max(s0, axis=0, keepdims=True) - off0, jnp.max(s1, axis=0, keepdims=True) - off1)
        m = jnp.maximum(m_old, top)
        m_ref[:, cols] = m
        p0 = jnp.exp2(s0 - (m + off0)).astype(BF16)
        p1 = jnp.exp2(s1 - (m + off1)).astype(BF16)
        p = jnp.concatenate([p0, p1], axis=0)
        new = jnp.dot(vb[slot, 0:ACC, :], p, preferred_element_type=F32)
        acc[:, cols] = acc[:, cols] * jnp.exp2(m_old - m) + new

    relay(1)
    ready(0, 0)
    scores(slot_of(0), 0, 0)

    steps = 8 - TAIL

    @pl.loop(0, 2 * steps)
    def _(hs):
        step = hs // 2
        odd = hs % 2

        for n in range(steps):
            @pl.when(hs == 2 * n + 1)
            def _(n=n):
                if n <= 3:
                    relay_y(n + 1)
                if n <= 2:
                    relay(n + 2)
                ready(n + 1, 0)

            @pl.when(hs == 2 * n)
            def _(n=n):
                ready(n, 1)

        slot = slot_of(step)
        ends = ends_of(step)
        scores(slot, 2 * odd + 1, 1)
        update(slot, 2 * odd, 0, ends)
        scores(slot_of(step + odd), 2 - 2 * odd, 0)
        update(slot, 2 * odd + 1, 1, ends)

    def tail_step(step):
        if step == 6:
            return 6, ends_6
        if step == 7:
            return 7, ends_7
        return slot_of(step), ends_of(step)

    def rs_copy(src, dst, number, mate):
        return pltpu.make_async_remote_copy(
            src_ref=src, dst_ref=dst, send_sem=rs_send.at[number], recv_sem=rs_recv.at[number],
            device_id=mate, device_id_type=MESH)

    far = (x + 2) % 4
    after = (x + 1) % 4
    before = (x + 3) % 4

    def first(r):
        return (rs_copy(part.at[r, 2 * far + 1], ra.at[r, 0], 5 * r, x_next),
                rs_copy(part.at[r, 2 * far], ra.at[r, 1], 5 * r + 1, x_prev))

    def second(r):
        return (rs_copy(part.at[r, pl.ds(2 * after, 2)], rb.at[r, 0], 5 * r + 2, x_next),
                rs_copy(part.at[r, pl.ds(2 * before, 2)], rb.at[r, 1], 5 * r + 3, x_prev))

    def third(r):
        return rs_copy(cb.at[r], rc.at[r], 5 * r + 4, yh_mate)

    def pass_first(r):
        got = first(r)
        onward = second(r)
        for n, block in ((0, 2 * after + 1), (1, 2 * before)):
            got[n].wait_recv()
            part[r, block] = (part[r, block].astype(F32) + ra[r, n].astype(F32)).astype(BF16)
            onward[n].start()

    def pass_second(r):
        for copy in second(r):
            copy.wait_recv()
        for keep in range(2):
            block = yh if keep else 1 - yh
            total = (part[r, 2 * x + block].astype(F32) + rb[r, 0, block].astype(F32)
                     + rb[r, 1, block].astype(F32))
            if keep:
                fb[r] = total
            else:
                cb[r] = total.astype(BF16)
                third(r).start()

    def pass_third(r):
        third(r).wait_recv()
        rows = pl.ds(pl.multiple_of(r * CHUNK, CHUNK), CHUNK)
        out_ref[rows, :] = (fb[r] + rc[r].astype(F32)).astype(BF16)

    load_w.wait()

    @pl.loop(0, CHUNKS)
    def _(r):
        for n in range(TAIL):
            step = 8 - TAIL + n
            if n < TAIL - 1:
                @pl.when(r == 0)
                def _(step=step):
                    ready(step, 1)
                    ready(step + 1, 0)
                scores(tail_step(step + 1)[0], r, (n + 1) % 2)
            else:
                @pl.when(r == 0)
                def _(step=step):
                    ready(step, 1)
                scores(tail_step(8 - TAIL)[0], (r + 1) % CHUNKS, 0)
            slot, ends = tail_step(step)
            update(slot, r, n % 2, ends)

        @pl.when(r >= 1)
        def _():
            pass_first(r - 1)

        cols = pl.ds(pl.multiple_of(r * WIDE, WIDE), WIDE)
        done = (acc[0:HEAD, cols] / acc[HEAD:HEAD + 1, cols]).astype(BF16)
        for h in range(HEADS):
            att[:, h * HEAD:(h + 1) * HEAD] = done[:, h * CHUNK:(h + 1) * CHUNK].T
        for n, step in enumerate((1, 0, 2, 3, 4, 5, 6, 7)):
            block = (2 * far + step) % 8
            at = pl.multiple_of(block * COLS, COLS)
            part[r, block] = jnp.dot(att[...], w_buf[:, pl.ds(at, COLS)],
                                     preferred_element_type=F32).astype(BF16)
            if n < 2:
                first(r)[n].start()

        @pl.when(r >= 2)
        def _():
            pass_second(r - 2)

    pass_first(CHUNKS - 1)
    pass_second(CHUNKS - 2)
    pass_third(0)
    pass_third(1)
    pass_second(CHUNKS - 1)
    pass_third(2)
    pass_third(3)

    for number in range(16):
        for n in range(2):
            part_copy(own, 0, 0, number, core, n).wait_send()
    for r in range(CHUNKS):
        for copy in (*first(r), *second(r), third(r)):
            copy.wait_send()


def local(queries, stacked_keys, stacked_values, doc_start, out_weight):
    vmem = pl.BlockSpec(memory_space=pltpu.VMEM)
    anywhere = pl.BlockSpec(memory_space=pl.ANY)
    return pl.pallas_call(
        kernel,
        out_shape=jax.ShapeDtypeStruct((ROWS, COLS), BF16),
        in_specs=[anywhere, vmem, vmem, vmem, anywhere],
        out_specs=vmem,
        scratch_shapes=[
            pltpu.VMEM((ROWS, HEADS * HEAD), BF16),
            pltpu.VMEM((HEADS * HEAD, 8 * COLS), BF16),
            pltpu.VMEM((CHUNKS * WIDE, 2 * HEAD), BF16),
            pltpu.VMEM((ROWS, HEAD), BF16),
            pltpu.VMEM((VROWS, ROWS), BF16),
            pltpu.VMEM((VROWS, ROWS), BF16),
            pltpu.VMEM((8, PAIR, HEAD), BF16),
            pltpu.VMEM((8, VROWS, PAIR), BF16),
            pltpu.VMEM((2, PAIR, WIDE), F32),
            pltpu.VMEM((1, CHUNKS * WIDE), F32),
            pltpu.VMEM((ACC, CHUNKS * WIDE), F32),
            pltpu.VMEM((CHUNK, HEADS * HEAD), BF16),
            pltpu.VMEM((CHUNKS, 8, CHUNK, COLS), BF16),
            pltpu.VMEM((CHUNKS, 2, CHUNK, COLS), BF16),
            pltpu.VMEM((CHUNKS, 2, 2, CHUNK, COLS), BF16),
            pltpu.VMEM((CHUNKS, CHUNK, COLS), BF16),
            pltpu.VMEM((CHUNKS, CHUNK, COLS), BF16),
            pltpu.VMEM((CHUNKS, CHUNK, COLS), F32),
            pltpu.SemaphoreType.DMA((2,)),
            pltpu.SemaphoreType.DMA((32,)),
            pltpu.SemaphoreType.DMA((32,)),
            pltpu.SemaphoreType.DMA((5 * CHUNKS,)),
            pltpu.SemaphoreType.DMA((5 * CHUNKS,)),
        ],
        compiler_params=pltpu.CompilerParams(
            collective_id=0, has_side_effects=True, vmem_limit_bytes=60 << 20),
        name="attend_and_project",
    )(queries, stacked_keys, stacked_values, doc_start.reshape(CHUNKS, CHUNK), out_weight)


def solution(mesh):
    from jax.sharding import PartitionSpec as P

    return jax.shard_map(
        local,
        mesh=mesh,
        in_specs=(P("ctx", "tp"), P("ctx", "tp"), P("ctx", "tp"), P("ctx"), P("tp", None)),
        out_specs=P("ctx", "tp"),
        check_vma=False,
    )
```
